32 devices in a mesh: col: 8 (over z, x), row: 4 (over y, core).
Axes of the slice: x: 2, y: 2, z: 4, core: 2. Of those that a mesh axis runs over, the one named last changes fastest.
Arguments:
- vorticity: float32 [2, 8, 1024, 2048], P(None, 'row', 'col'), may hold values from -0.0017578125 to 0.0017578125
- divergence: float32 [2, 8, 1024, 2048], P(None, 'row', 'col'), may hold values from -0.0017578125 to 0.0017578125
- trunc_cut: int32 [1024], P('col'), may hold values from -1 to 1023, as said below
- level_slot: int32 [8], replicated, may hold values from 0 to 7, each once
Outputs:
- u_wind: float32 [8, 2048, 2048], P(None, ('col', 'row'))
- v_wind: float32 [8, 2048, 2048], P(None, ('col', 'row'))
- u_slope: float32 [8, 2048, 2048], P(None, ('col', 'row'))
- v_slope: float32 [8, 2048, 2048], P(None, ('col', 'row'))
The draws below stay inside these ranges and needn't reach their ends.
Inputs may be any that keep to these rules, and one draw needn't show every extreme that they name: trunc_cut never rises with m, is 1023 at m = 0 and -1 (nothing kept) at the last m. level_slot is a permutation of the model levels.
All inputs are finite; a program needn't handle non-finite values.
Results may differ from the reference program's by a relative error of at most 0.0001.
Values sent between devices are 32-bit elements; how exact they have to be, the bound alone decides.
A program may use at most 128 MiB of HBM per device.

```python
import math
import jax
import jax.numpy as jnp
from jax import lax

NX = 2048
NY = 2048
MX = 1024
LEVELS = 8


def draw_trunc_cut(key, part):
    first_key = jax.random.fold_in(key, 11)
    second_key = jax.random.fold_in(key, 23)
    wave_axis = jax.random.randint(first_key, (), 3 * MX // 4, MX - 1)
    north_axis = jax.random.randint(second_key, (), 3 * (NY // 2) // 4, NY // 2)
    wave_index = jnp.arange(MX, dtype=jnp.int32)
    north_index = jnp.arange(NY // 2, dtype=jnp.int32)
    scaled = wave_index * north_axis // wave_axis
    inside = north_index[None, :] * north_index[None, :] + scaled[:, None] * scaled[:, None] <= north_axis * north_axis
    counted = jnp.sum(inside.astype(jnp.int32), axis=1) - 1
    shaped = jnp.where(wave_index > wave_axis, -1, counted)
    return jnp.where(wave_index == 0, NY // 2 - 1, shaped).astype(jnp.int32)


def level_of(stream_key, dims, split, low, top_value):
    gain, own = 1.0, jax.random.fold_in(stream_key, 6)
    for axis_at, blocks in split:
        draws = jnp.exp(jax.random.uniform(jax.random.fold_in(own, axis_at), (blocks,), jnp.float32, low / len(split), top_value / len(split)))
        gain = gain * jnp.repeat(draws, dims[axis_at] // blocks).reshape([-1 if axis == axis_at else 1 for axis in range(len(dims))])
    return gain


def centred(rng, dims, deviation, bound, shards=(), kind=jnp.bfloat16):
    gain = level_of(rng, dims, shards, -0.22, 0.18) if shards else 1.0
    drawn = jax.random.normal(rng, dims, jnp.float32) * deviation * gain
    return jnp.minimum(jnp.maximum(drawn, -bound), bound).astype(kind)


def setup_inputs(seed: int = 0) -> dict:
    key_of = jax.random.split(jax.random.key(seed), 5)
    return {
        "vorticity": centred(key_of[0], (2, LEVELS, MX, NY), (0.6 * NX ** -1), 0.0017578125, ((1, 4), (2, 8)), jnp.float32),
        "divergence": centred(key_of[1], (2, LEVELS, MX, NY), (0.6 * NX ** -1), 0.0017578125, ((1, 4), (2, 8)), jnp.float32),
        "trunc_cut": draw_trunc_cut(jax.random.fold_in(key_of[4], 71), 0),
        "level_slot": jax.random.permutation(key_of[3], LEVELS).astype(jnp.int32),
    }


def reference(vorticity, divergence, trunc_cut, level_slot):
    wave_index = jnp.arange(NX // 2, dtype=jnp.int32)
    north_index = jnp.arange(NY, dtype=jnp.int32)
    north_wave = jnp.where(north_index < NY // 2, north_index, north_index - NY)
    wave_east = (2.0 * math.pi / NX) * wave_index.astype(jnp.float32)
    wave_north = (2.0 * math.pi / NY) * north_wave.astype(jnp.float32)
    east_col = wave_east[:, None]
    north_row = wave_north[None, :]
    square_wave = east_col * east_col + north_row * north_row
    retained = (jnp.abs(north_wave)[None, :] <= trunc_cut[:, None]) & (square_wave > 0)
    inverse_square = jnp.where(retained, 1.0 / jnp.where(square_wave > 0, square_wave, 1.0), 0.0)
    weights = jnp.where(wave_index == 0, 1.0, 2.0).astype(jnp.float32)

    def one_level(slot_data):
        curl_real, curl_imag, source_real, source_imag = slot_data
        east_real = (-north_row * curl_imag + east_col * source_imag) * inverse_square
        east_imag = (north_row * curl_real - east_col * source_real) * inverse_square
        north_real = (east_col * curl_imag + north_row * source_imag) * inverse_square
        north_imag = (-east_col * curl_real - north_row * source_real) * inverse_square
        results = []
        for real_part, imag_part in ((east_real, east_imag), (north_real, north_imag)):
            coeffs = real_part + 1j * imag_part
            meridional = jnp.fft.ifft(coeffs, axis=1) * NY
            weighted = meridional * weights[:, None]
            padded = jnp.concatenate([weighted, jnp.zeros_like(weighted)], axis=0)
            value_grid = (jnp.fft.ifft(padded, axis=0) * NX).real.T
            sloped = jnp.concatenate([weighted * (1j * wave_east[:, None]), jnp.zeros_like(weighted)], axis=0)
            slope_grid = (jnp.fft.ifft(sloped, axis=0) * NX).real.T
            results.append(value_grid)
            results.append(slope_grid)
        return tuple(results)

    values = lax.map(one_level, (vorticity[0], vorticity[1], divergence[0], divergence[1]))
    inverse = jnp.argsort(level_slot).astype(jnp.int32)
    return (values[0][inverse], values[2][inverse], values[1][inverse], values[3][inverse])
```

```python
import math

import jax
import jax.numpy as jnp
import numpy as np
from jax import lax
from jax.sharding import PartitionSpec as P

HIGH = lax.Precision.HIGH


def split_waves(array, axis):
    first = lax.slice_in_dim(array, 0, None, 2, axis)
    second = lax.slice_in_dim(array, 1, None, 2, axis)
    return jnp.concatenate([first, second], axis)


def phases(product, period):
    angles = 2.0 * np.pi * (product % period) / period
    return np.cos(angles).astype(np.float32), np.sin(angles).astype(np.float32)


def multiply(first, second):
    return first[0] * second[0] - first[1] * second[1], first[0] * second[1] + first[1] * second[0]


def north_table(north_cells):
    quarter = north_cells // 4
    fine = math.gcd(quarter, 32)
    column = np.arange(quarter)
    coarse_row = 4 * fine * np.arange(quarter // fine)[None, :, None, None] + np.arange(4)[:, None, None, None]
    fine_row = 4 * np.arange(fine)[None, None, :, None]
    coarse = phases(coarse_row * column, north_cells)
    close = phases(fine_row * column, north_cells)
    coarse, close = lax.optimization_barrier((coarse, close))
    cosine, sine = multiply(coarse, close)
    joined = jnp.concatenate([cosine, -sine], axis=3)
    return joined.reshape(4, quarter, 2 * quarter)


def east_table(columns, local_waves, east_cells):
    half = local_waves // 2
    cells = east_cells // 2
    column = np.arange(cells)
    coarse_wave = np.arange(2)[:, None, None, None] + local_waves * np.arange(columns)[None, :, None, None]
    close_wave = 2 * np.arange(half)[None, None, :, None]
    coarse = phases(coarse_wave * column, east_cells)
    close = phases(close_wave * column, east_cells)
    coarse, close = lax.optimization_barrier((coarse, close))
    cosine, sine = multiply(coarse, close)
    wave = coarse_wave + close_wave
    weights = np.where(wave == 0, 1.0, 2.0).astype(np.float32)
    scaled = (weights * wave * (2.0 * np.pi / east_cells)).astype(np.float32)
    real = jnp.concatenate([weights * cosine, -scaled * sine], axis=3)
    imag = jnp.concatenate([-weights * sine, -scaled * cosine], axis=3)
    joined = jnp.stack([real, imag], axis=2)
    return joined.reshape(2, columns * local_waves, 2 * cells)


def spectral_winds(vorticity, divergence, trunc_cut, wave_index, east_cells):
    north_cells = vorticity.shape[3]
    north_index = jnp.arange(north_cells, dtype=jnp.int32)
    north_wave = jnp.where(north_index < north_cells // 2, north_index, north_index - north_cells)
    wave_east = 2.0 * math.pi / east_cells * wave_index.astype(jnp.float32)
    wave_north = 2.0 * math.pi / north_cells * north_wave.astype(jnp.float32)
    east_col = wave_east[:, None]
    north_row = wave_north[None, :]
    square_wave = east_col * east_col + north_row * north_row
    retained = (jnp.abs(north_wave)[None, :] <= trunc_cut[:, None]) & (square_wave > 0)
    inverse_square = jnp.where(retained, 1.0 / jnp.where(square_wave > 0, square_wave, 1.0), 0.0)
    east_inverse = east_col * inverse_square
    north_inverse = north_row * inverse_square
    curl_real, curl_imag = vorticity[0], vorticity[1]
    source_real, source_imag = divergence[0], divergence[1]
    east = (
        -north_inverse * curl_imag + east_inverse * source_imag,
        north_inverse * curl_real - east_inverse * source_real,
    )
    north = (
        east_inverse * curl_imag + north_inverse * source_imag,
        -east_inverse * curl_real - north_inverse * source_real,
    )
    return east, north


def fold_quarters(wind, slots, half):
    real, imag = wind
    quarter = real.shape[2] // 4
    r0, r1, r2, r3 = (real[:, :, q * quarter:(q + 1) * quarter] for q in range(4))
    i0, i1, i2, i3 = (imag[:, :, q * quarter:(q + 1) * quarter] for q in range(4))
    folded = (
        (r0 + r2 + (r1 + r3), i0 + i2 + (i1 + i3)),
        (r0 - r2 - (i1 - i3), i0 - i2 + (r1 - r3)),
        (r0 + r2 - (r1 + r3), i0 + i2 - (i1 + i3)),
        (r0 - r2 + (i1 - i3), i0 - i2 - (r1 - r3)),
    )
    parts = []
    for part_real, part_imag in folded:
        shape = (slots, 2, 1, half, 2 * quarter)
        top = jnp.concatenate([part_real, part_imag], axis=2).reshape(shape)
        low = jnp.concatenate([part_imag, -part_real], axis=2).reshape(shape)
        parts.append(jnp.concatenate([top, low], axis=2))
    return jnp.stack(parts, axis=0).reshape(4, slots * 4 * half, 2 * quarter)


def on_device(vorticity, divergence, trunc_cut, level_slot):
    columns = lax.axis_size("col")
    row_devices = lax.axis_size("row")
    slots, local_waves, north_cells = vorticity.shape[1:]
    half = local_waves // 2
    quarter = north_cells // 4
    levels = slots * row_devices
    east_cells = 2 * local_waves * columns
    cells = east_cells // 2
    block = quarter // (columns * row_devices)
    first_wave = lax.axis_index("col") * local_waves
    wave_index = first_wave + jnp.arange(local_waves, dtype=jnp.int32)
    winds = spectral_winds(
        split_waves(vorticity, 2),
        split_waves(divergence, 2),
        split_waves(trunc_cut, 0),
        split_waves(wave_index, 0),
        east_cells,
    )
    table_north = north_table(north_cells)
    table_east = east_table(columns, local_waves, east_cells)
    holder = jnp.argsort(level_slot).astype(jnp.int32)
    results = []
    for wind in winds:
        folded = fold_quarters(wind, slots, half)
        fourier = jnp.einsum("pjk,pmk->pjm", table_north, folded, precision=HIGH)
        outgoing = fourier.reshape(4, quarter, slots, 2 * local_waves).transpose(1, 2, 0, 3)
        received = lax.all_to_all(outgoing, ("col", "row"), split_axis=0, concat_axis=0, tiled=True)
        shaped = received.reshape(columns, row_devices, block, slots, 4, 2, local_waves)
        arranged = shaped.transpose(1, 3, 5, 2, 4, 0, 6).reshape(
            levels, 2, block * 4, columns * local_waves
        )
        placed = jnp.concatenate(
            [lax.dynamic_slice_in_dim(arranged, holder[level], 1, 0) for level in range(levels)], axis=0
        )
        even = jnp.einsum("lyk,kx->lyx", placed[:, 0], table_east[0], precision=HIGH)
        odd = jnp.einsum("lyk,kx->lyx", placed[:, 1], table_east[1], precision=HIGH)
        total, rest = even + odd, even - odd
        results.append(
            (
                jnp.concatenate([total[:, :, :cells], rest[:, :, :cells]], axis=2),
                jnp.concatenate([total[:, :, cells:], rest[:, :, cells:]], axis=2),
            )
        )
    return results[0][0], results[1][0], results[0][1], results[1][1]


def solution(mesh):
    return jax.shard_map(
        on_device,
        mesh=mesh,
        in_specs=(P(None, "row", "col", None), P(None, "row", "col", None), P("col"), P()),
        out_specs=(
            P(None, ("col", "row"), None),
            P(None, ("col", "row"), None),
            P(None, ("col", "row"), None),
            P(None, ("col", "row"), None),
        ),
        check_vma=False,
    )
```
